128 devices in a mesh: depth: 4 (over x), probe: 32 (over z, y, core).
Axes of the slice: x: 4, y: 4, z: 4, core: 2. Of those that a mesh axis runs over, the one named last changes fastest.
Arguments:
- atom_blocks: bfloat16 [4, 4096, 128, 128], P('depth', 'probe'), may hold values from 0 to 1.5
- atom_tile: int32 [4, 4096], P('depth', 'probe'), may hold values from 0 to 1023, as said below
- slice_counts: int32 [4], P('depth'), may hold values from 1 to 4, as said below
- positions: int32 [128], P('probe'), may hold values from 0 to 7, as said below
- probe_wave: float32 [2, 256, 256], replicated, may hold values from -4 to 4
- prop_phase: float32 [256, 256], replicated, may hold values from -3.140625 to 3.140625
Outputs:
- exit_waves: float32 [4, 128, 2, 256, 256], P('depth', 'probe')
The draws below stay inside these ranges and needn't reach their ends.
Inputs may be any that keep to these rules, and one draw needn't show every extreme that they name: `atom_tile`: tile number owner * 32 + s * 8 + c names tile row owner, slice slot s and tile column c, with s below slice_counts of that section. In each section the 128 atoms of one index of probe (aligned blocks) name at most 6 tiles of any one tile row, and in every draw each section has a tile row that receives exactly 6 from every such block. `slice_counts`: some section has exactly 4 slices in every draw. The 4 probes of one tile row (aligned blocks of 4) have distinct positions.
All inputs are finite; a program needn't handle non-finite values.
Results may differ from the reference program's by a relative error of at most 0.04.
Values may be sent and summed in bfloat16 or wider, within the bound.
No kernel may reach another device: no remote copies, remote signals or barrier semaphores. Data moves between devices by JAX's collectives and lax.ppermute only.
A program may use at most 128 MiB of HBM per device.

```python
import math
import jax
import jax.numpy as jnp
from jax import lax

TILE = 128
SLICE_MAX = 4
TCOLS = 8
WAVES_DEV = 4
ATOMS_DEV = 128
N = 256
SECTIONS = 4
PROBES = 128
ATOMS = 4096
ROWS = 4096
COLS = 1024
TILES_DEV = 32
CAP = 6
N_PROBE = 32


def layout(key):
    draws = jax.random.randint(jax.random.fold_in(key, 101), (SECTIONS,), 1, SLICE_MAX + 1)
    full_at = jax.random.randint(jax.random.fold_in(key, 102), (), 0, SECTIONS)
    counts = draws.at[full_at].set(SLICE_MAX).astype(jnp.int32)
    owners = ATOMS // ATOMS_DEV
    hot_owner = jax.random.randint(jax.random.fold_in(key, 103), (SECTIONS,), 0, owners)
    remaining = ATOMS_DEV - CAP
    base_key = jax.random.fold_in(key, 104)

    def one_block(block_key, busy_owner, slice_limit):
        chosen = jax.random.permutation(jax.random.fold_in(block_key, 1), (owners - 1) * CAP)[:remaining]
        elsewhere = (chosen // CAP).astype(jnp.int32)
        elsewhere = elsewhere + (elsewhere >= busy_owner).astype(jnp.int32)
        owner_of = jnp.concatenate([jnp.full((CAP,), busy_owner, jnp.int32), elsewhere])
        owner_of = jax.random.permutation(jax.random.fold_in(block_key, 2), owner_of)
        slice_pick = jax.random.randint(jax.random.fold_in(block_key, 3), (ATOMS_DEV,), 0, slice_limit)
        col_pick = jax.random.randint(jax.random.fold_in(block_key, 4), (ATOMS_DEV,), 0, TCOLS)
        return (owner_of * TILES_DEV + slice_pick * TCOLS + col_pick).astype(jnp.int32)

    def one_section(section_index):

        def one_source(source_index):
            block_key = jax.random.fold_in(base_key, section_index * owners + source_index)
            return one_block(block_key, hot_owner[section_index], counts[section_index])
        return jax.vmap(one_source)(jnp.arange(owners, dtype=jnp.int32)).reshape(ATOMS)
    tiles = jax.vmap(one_section)(jnp.arange(SECTIONS, dtype=jnp.int32))
    return (counts, tiles.astype(jnp.int32))


def draw_slice_counts(key, part):
    return layout(key)[0]


def draw_atom_tile(key, part):
    return layout(key)[1]


def draw_positions(key, part):
    groups = PROBES // WAVES_DEV
    base_key = jax.random.fold_in(key, 200)

    def one_group(group_index):
        order = jax.random.permutation(jax.random.fold_in(base_key, group_index), jnp.arange(TCOLS, dtype=jnp.int32))
        return order[:WAVES_DEV]
    rows = jax.vmap(one_group)(jnp.arange(groups, dtype=jnp.int32))
    middle = 1 + jax.random.permutation(jax.random.fold_in(key, 300), jnp.arange(TCOLS - 2, dtype=jnp.int32))
    head = jnp.concatenate([jnp.array([0, TCOLS - 1], jnp.int32), middle])[:WAVES_DEV]
    head = jax.random.permutation(jax.random.fold_in(key, 301), head)
    rows = rows.at[0].set(head)
    return rows.reshape(PROBES).astype(jnp.int32)


def block_levels(rng, dims, cuts, smallest, largest):
    gain, own = 1.0, jax.random.fold_in(rng, 6)
    for dim, parts in cuts:
        steps = jnp.exp(jax.random.uniform(jax.random.fold_in(own, dim), (parts,), jnp.float32, smallest / len(cuts), largest / len(cuts)))
        gain = gain * jnp.repeat(steps, dims[dim] // parts).reshape([-1 if axis == dim else 1 for axis in range(len(dims))])
    return gain


def scatter_about(rng, dims, width, limit, held_as=jnp.bfloat16):
    values = width * jax.random.normal(rng, dims, jnp.float32)
    return jnp.clip(values, min=-limit, max=limit).astype(held_as)


def setup_inputs(seed: int = 0) -> dict:
    splits = jax.random.split(jax.random.key(seed), 7)
    atom_blocks = jnp.clip(1.5 * jax.random.uniform(splits[0], (SECTIONS, ATOMS, TILE, TILE), jnp.float32) ** block_levels(splits[0], (SECTIONS, ATOMS, TILE, TILE), ((0, 4), (1, 32)), -0.2, 0.2), 0.0, 1.5).astype(jnp.bfloat16)
    atom_tile = draw_atom_tile(jax.random.fold_in(splits[6], 71), 0)
    slice_counts = draw_slice_counts(jax.random.fold_in(splits[6], 71), 0)
    positions = draw_positions(jax.random.fold_in(splits[6], 71), 0)
    probe_wave = scatter_about(splits[4], (2, N, N), 0.5, 4.0, jnp.float32)
    prop_phase = jnp.clip(jax.random.uniform(splits[5], (N, N), jnp.float32, -3.140625, 3.140625), -3.140625, 3.140625)
    return dict(atom_blocks=atom_blocks, atom_tile=atom_tile, slice_counts=slice_counts, positions=positions, probe_wave=probe_wave, prop_phase=prop_phase)


SIGMA = 0.7

def dft_tables(points):
    grid_index = jnp.arange(points, dtype=jnp.int32)
    angle_table = (grid_index[:, None] * grid_index[None, :] % points).astype(jnp.float32) * (2.0 * math.pi / points)
    norm_scale = 1.0 / math.sqrt(points)
    real_part = (jnp.cos(angle_table) * norm_scale).astype(jnp.bfloat16)
    imag_part = (-jnp.sin(angle_table) * norm_scale).astype(jnp.bfloat16)
    return (real_part, imag_part)

def left_apply(real_part, imag_part, field):
    field = field.astype(jnp.float32)
    first_term = jnp.einsum('jk,bckl->bcjl', real_part.astype(jnp.float32), field, precision=lax.Precision.HIGHEST)
    second_term = jnp.einsum('jk,bckl->bcjl', imag_part.astype(jnp.float32), field, precision=lax.Precision.HIGHEST)
    return jnp.stack([first_term[:, 0] - second_term[:, 1], first_term[:, 1] + second_term[:, 0]], axis=1)

def right_apply(real_part, imag_part, field):
    field = field.astype(jnp.float32)
    first_term = jnp.einsum('bcjk,kl->bcjl', field, real_part.astype(jnp.float32), precision=lax.Precision.HIGHEST)
    second_term = jnp.einsum('bcjk,kl->bcjl', field, imag_part.astype(jnp.float32), precision=lax.Precision.HIGHEST)
    return jnp.stack([first_term[:, 0] - second_term[:, 1], first_term[:, 1] + second_term[:, 0]], axis=1)

def to_bf16(values):
    return lax.optimization_barrier(values.astype(jnp.bfloat16))

def slice_step(wave, cropped, real_part, imag_part, rotor_cos, rotor_sin):
    cosine = jnp.cos(SIGMA * cropped)
    sine_part = jnp.sin(SIGMA * cropped)
    wave_re = wave[:, 0]
    wave_im = wave[:, 1]
    passed = to_bf16(jnp.stack([wave_re * cosine - wave_im * sine_part, wave_re * sine_part + wave_im * cosine], axis=1))
    spectrum = to_bf16(left_apply(real_part, imag_part, passed))
    spectral = right_apply(real_part, imag_part, spectrum)
    propagated = to_bf16(jnp.stack([spectral[:, 0] * rotor_cos - spectral[:, 1] * rotor_sin, spectral[:, 0] * rotor_sin + spectral[:, 1] * rotor_cos], axis=1))
    returned = to_bf16(left_apply(real_part, -imag_part, propagated))
    return right_apply(real_part, -imag_part, returned)

def reference(atom_blocks, atom_tile, slice_counts, positions, probe_wave, prop_phase):
    real_part, imag_part = dft_tables(N)
    rotor_cos = jnp.cos(prop_phase)
    rotor_sin = jnp.sin(prop_phase)
    grid_index = jnp.arange(N, dtype=jnp.int32)
    groups = jnp.arange(PROBES, dtype=jnp.int32) // WAVES_DEV
    row_index = (groups[:, None] * TILE - TILE // 2 + grid_index[None, :]) % ROWS
    col_index = (positions[:, None].astype(jnp.int32) * TILE + grid_index[None, :]) % COLS
    wave = jnp.broadcast_to(probe_wave[None], (PROBES, 2, N, N)).astype(jnp.float32)
    collected = []
    for section in range(SECTIONS):
        flat = atom_blocks[section].astype(jnp.float32).reshape(ATOMS, TILE * TILE)
        summed = jax.ops.segment_sum(flat, atom_tile[section], num_segments=N_PROBE * TILES_DEV)
        field = summed.reshape(N_PROBE, SLICE_MAX, TCOLS, TILE, TILE).transpose(1, 0, 3, 2, 4).reshape(SLICE_MAX, ROWS, COLS)

        def one_slice(slice_index, current, field=field):
            plane = lax.dynamic_index_in_dim(field, slice_index, 0, keepdims=False)
            cropped = plane[row_index[:, :, None], col_index[:, None, :]]
            return slice_step(current, cropped, real_part, imag_part, rotor_cos, rotor_sin)
        wave = lax.fori_loop(0, slice_counts[section], one_slice, wave)
        collected.append(wave)
    return jnp.stack(collected, axis=0)
```

```python
import functools
import math

import jax
import jax.numpy as jnp
from jax import lax
from jax.experimental import pallas as pl
from jax.experimental.pallas import tpu as pltpu
from jax.sharding import PartitionSpec as P

SLICE_MAX = 4
TCOLS = 8
TILES = SLICE_MAX * TCOLS
TILE = 128
N = 256
SIGMA = 0.7
CAP = 6
META = 16
POS_LANE = 8
CHUNKS = 2
ROWS = TILE // CHUNKS
SKIP = 64.0

BF16 = jnp.bfloat16
F32 = jnp.float32


def dft_tables(points):
    grid_index = jnp.arange(points, dtype=jnp.int32)
    angle_table = (grid_index[:, None] * grid_index[None, :] % points).astype(F32) * (
        2.0 * math.pi / points
    )
    norm_scale = 1.0 / math.sqrt(points)
    real_part = (jnp.cos(angle_table) * norm_scale).astype(BF16)
    imag_part = (-jnp.sin(angle_table) * norm_scale).astype(BF16)
    return (real_part, imag_part)


def whole(space=pltpu.VMEM):
    return pl.BlockSpec(memory_space=space)


def pack_kernel(row0, tile_sm, pos_sm, blocks_hbm, tile_row, tile_col, out, counts, sem):
    owners, rows_all, _ = out.shape
    atoms = tile_row.shape[1]

    @pl.loop(0, owners)
    def _(o):
        counts[o] = 0

    @pl.loop(0, atoms)
    def _(a):
        o = tile_sm[a] // TILES
        r = counts[o]
        counts[o] = r + 1
        pltpu.make_async_copy(
            blocks_hbm.at[a, pl.ds(row0, ROWS), :],
            out.at[o, pl.ds(pl.multiple_of(r * ROWS, ROWS), ROWS), :],
            sem,
        ).start()

    t_row = tile_row[...]
    t_col = tile_col[...]
    own_row = t_row // TILES
    own_col = t_col // TILES
    shape = (atoms, atoms)
    i_sub = lax.broadcasted_iota(jnp.int32, shape, 0)
    i_lane = lax.broadcasted_iota(jnp.int32, shape, 1)
    earlier = jnp.where((own_row == own_col) & (i_lane < i_sub), 1.0, 0.0)
    rank_col = jnp.sum(earlier, axis=1, keepdims=True).astype(jnp.int32)
    slot_of = jnp.where(rank_col == i_lane, (t_col % TILES + 1).astype(F32), 0.0).astype(BF16)
    o_sub = lax.broadcasted_iota(jnp.int32, (owners, atoms), 0)
    o_lane = lax.broadcasted_iota(jnp.int32, (owners, atoms), 1)
    named = jnp.where(own_row == o_sub, 1.0, 0.0).astype(BF16)
    meta = jnp.dot(named, slot_of, preferred_element_type=F32)
    for k in range(pos_sm.shape[0]):
        meta = jnp.where(o_lane == POS_LANE + k, pos_sm[k].astype(F32), meta)
    for o in range(owners):
        line = jnp.broadcast_to(meta[o : o + 1, :], (META, atoms))
        out[o, pl.ds(CAP * ROWS, META), :] = line.astype(BF16)
    pltpu.make_async_copy(
        blocks_hbm.at[:, pl.ds(row0, ROWS), :], blocks_hbm.at[:, pl.ds(row0, ROWS), :], sem
    ).wait()


def pack(blocks, tiles, positions, chunk, owners):
    atoms = blocks.shape[0]
    return pl.pallas_call(
        functools.partial(pack_kernel, chunk * ROWS),
        out_shape=jax.ShapeDtypeStruct((owners, CAP * ROWS + META, TILE), BF16),
        in_specs=[whole(pltpu.SMEM), whole(pltpu.SMEM), whole(pl.ANY), whole(), whole()],
        out_specs=whole(),
        scratch_shapes=[pltpu.SMEM((owners,), jnp.int32), pltpu.SemaphoreType.DMA],
        name=f"pack{chunk}",
    )(tiles, positions, blocks, tiles.reshape(1, atoms), tiles.reshape(atoms, 1))


TWO_PI_HI = 6.28125
TWO_PI_LO = 2.0 * math.pi - TWO_PI_HI


def gather_kernel(upper, slices_sm, place_sm, arrived, own, halo, acc, meta_v, meta_s, sem):
    owners = arrived.shape[0]
    waves = own.shape[0]
    meta_v[...] = arrived[:, CAP * ROWS, :].astype(F32).astype(jnp.int32)
    copy = pltpu.make_async_copy(meta_v, meta_s, sem)
    copy.start()
    acc[...] = jnp.zeros_like(acc)
    copy.wait()

    @pl.loop(0, owners)
    def _(o):
        for r in range(CAP):
            t = meta_s[o, r]

            @pl.when(t > 0)
            def _():
                acc[t - 1] += arrived[o, pl.ds(r * ROWS, ROWS), :].astype(F32)

    count = slices_sm[0]
    me = place_sm[0]
    ahead = place_sm[1]

    def phase(tile):
        angle = SIGMA * acc[tile]
        turns = jnp.round(angle * (1.0 / (2.0 * math.pi)))
        return ((angle - turns * TWO_PI_HI) - turns * TWO_PI_LO).astype(BF16)

    for target, ref in ((me, own), (ahead, halo)):
        for d in range(waves):
            start = meta_s[target, POS_LANE + d]
            for h in range(2):
                column = lax.rem(start + h, TCOLS)

                @pl.loop(0, SLICE_MAX)
                def _(s):
                    value = phase(s * TCOLS + column)
                    ref[d, s, h] = jnp.where(s < count, value, jnp.full_like(value, SKIP))


def gather(arrived, slice_count, place, upper, waves, chunk):
    shape = jax.ShapeDtypeStruct((waves, SLICE_MAX, 2, ROWS, TILE), BF16)
    owners = arrived.shape[0]
    return pl.pallas_call(
        functools.partial(gather_kernel, upper),
        out_shape=(shape, shape),
        in_specs=[whole(pltpu.SMEM), whole(pltpu.SMEM), whole()],
        out_specs=(whole(), whole()),
        scratch_shapes=[
            pltpu.VMEM((TILES, ROWS, TILE), F32),
            pltpu.VMEM((owners, TILE), jnp.int32),
            pltpu.SMEM((owners, TILE), jnp.int32),
            pltpu.SemaphoreType.DMA,
        ],
        name=f"gather{chunk}",
    )(slice_count, place, arrived)


SIN_C = (-1.6666654611e-1, 8.3321608736e-3, -1.9515295891e-4)
COS_C = (4.166664568298827e-2, -1.388731625493765e-3, 2.443315711809948e-5)


def sin_cos(angle):
    quarter = jnp.round(angle * (2.0 / math.pi))
    x = angle - quarter * (math.pi / 2.0)
    x2 = x * x
    s = x + x * x2 * (SIN_C[0] + x2 * (SIN_C[1] + x2 * SIN_C[2]))
    c = 1.0 - 0.5 * x2 + x2 * x2 * (COS_C[0] + x2 * (COS_C[1] + x2 * COS_C[2]))
    odd = jnp.abs(quarter) == 1.0
    sin_out = jnp.where(odd, c, s)
    cos_out = jnp.where(odd, s, c)
    sin_out = jnp.where((quarter == -1.0) | (jnp.abs(quarter) == 2.0), -sin_out, sin_out)
    cos_out = jnp.where((quarter == 1.0) | (jnp.abs(quarter) == 2.0), -cos_out, cos_out)
    return sin_out, cos_out


def waves_kernel(sections, wave_ref, phase_ref, m1, m2, *refs):
    windows = refs[: 2 * CHUNKS]
    out, psi, left, mid, rotor = refs[2 * CHUNKS :]
    step = 32

    for b in range(N // step):
        rows = pl.ds(b * step, step)
        for c in range(2):
            psi[rows, pl.ds(c * N, N)] = wave_ref[c, rows, :]
        angle = phase_ref[rows, :]
        s_out, c_out = sin_cos(angle)
        rotor[rows, pl.ds(0, N)] = c_out
        rotor[rows, pl.ds(N, N)] = s_out

    def place_of(row):
        if row < TILE // 2:
            tile_row, base = row + TILE // 2, CHUNKS
        elif row < TILE // 2 + TILE:
            tile_row, base = row - TILE // 2, 0
        else:
            tile_row, base = row - TILE // 2 - TILE, CHUNKS
        return windows[base + tile_row // ROWS], tile_row % ROWS

    def one_slice(sec, s):
        for b in range(N // step):
            ref, row = place_of(b * step)
            rows = pl.ds(b * step, step)
            for h in range(2):
                angle = ref[sec, s, h, pl.ds(row, step), :].astype(F32)
                s_out, c_out = sin_cos(angle)
                re = psi[rows, pl.ds(h * TILE, TILE)]
                im = psi[rows, pl.ds(N + h * TILE, TILE)]
                lanes = pl.ds(h * TILE, TILE)
                left[rows, lanes] = (re * c_out - im * s_out).astype(BF16)
                left[pl.ds(N + b * step, step), lanes] = (re * s_out + im * c_out).astype(BF16)
        for c in range(2):
            half = jnp.dot(m1[pl.ds(c * N, N), :], left[...], preferred_element_type=F32)
            mid[:, pl.ds(c * N, N)] = half.astype(BF16)
        for b in range(2):
            half = N // 2
            rows = pl.ds(b * half, half)
            value = jnp.dot(mid[rows, :], m2[...], preferred_element_type=F32)
            re, im = value[:, :N], value[:, N:]
            cr, ci = rotor[rows, pl.ds(0, N)], rotor[rows, pl.ds(N, N)]
            left[rows, :] = (re * cr - im * ci).astype(BF16)
            left[pl.ds(N + b * half, half), :] = (re * ci + im * cr).astype(BF16)
        for c in range(2):
            half = jnp.dot(m2[pl.ds(c * N, N), :], left[...], preferred_element_type=F32)
            mid[:, pl.ds(c * N, N)] = half.astype(BF16)
        for b in range(2):
            half = N // 2
            rows = pl.ds(b * half, half)
            psi[rows, :] = jnp.dot(mid[rows, :], m1[...], preferred_element_type=F32)

    @pl.loop(0, sections)
    def _(sec):
        @pl.loop(0, SLICE_MAX)
        def _(s):
            used = jnp.max(windows[0][sec, s, 0, pl.ds(0, 16), :].astype(F32)) < SKIP / 2

            @pl.when(used)
            def _():
                one_slice(sec, s)

        for c in range(2):
            out[sec, c] = psi[:, pl.ds(c * N, N)].astype(BF16)


def run_waves(probe_wave, prop_phase, m1, m2, windows):
    sections = windows[0].shape[0]
    return pl.pallas_call(
        functools.partial(waves_kernel, sections),
        out_shape=jax.ShapeDtypeStruct((sections, 2, N, N), BF16),
        in_specs=[whole()] * (4 + len(windows)),
        out_specs=whole(),
        scratch_shapes=[
            pltpu.VMEM((N, 2 * N), F32),
            pltpu.VMEM((2 * N, N), BF16),
            pltpu.VMEM((N, 2 * N), BF16),
            pltpu.VMEM((N, 2 * N), F32),
        ],
        name="waves",
    )(probe_wave, prop_phase, m1, m2, *windows)


def shards(atom_blocks, atom_tile, slice_counts, positions, probe_wave, prop_phase):
    owners = lax.axis_size("probe")
    waves = positions.shape[0]
    me = lax.axis_index("probe")
    blocks = atom_blocks[0]
    tiles = atom_tile[0]
    up = [(i, (i + 1) % owners) for i in range(owners)]
    down = [(j, i) for i, j in up]
    own, halo = [], []
    for chunk in range(CHUNKS):
        upper = chunk * ROWS >= TILE // 2
        ahead = lax.rem(me + (1 if upper else owners - 1), owners)
        place = jnp.stack([me, ahead]).astype(jnp.int32)
        packed = pack(blocks, tiles, positions, chunk, owners)
        arrived = lax.all_to_all(packed, "probe", split_axis=0, concat_axis=0, tiled=True)
        mine, theirs = gather(arrived, slice_counts, place, upper, waves, chunk)
        mine = lax.all_to_all(mine, "depth", split_axis=0, concat_axis=0, tiled=True)
        theirs = lax.ppermute(theirs, "probe", up if upper else down)
        theirs = lax.all_to_all(theirs, "depth", split_axis=0, concat_axis=0, tiled=True)
        own.append(mine)
        halo.append(theirs)
    fr, fi = dft_tables(N)
    m1 = jnp.concatenate(
        [jnp.concatenate([fr, -fi], axis=1), jnp.concatenate([fi, fr], axis=1)], axis=0
    )
    m2 = jnp.concatenate(
        [jnp.concatenate([fr, fi], axis=1), jnp.concatenate([-fi, fr], axis=1)], axis=0
    )
    left = run_waves(probe_wave, prop_phase, m1, m2, own + halo)
    left = lax.all_to_all(left, "depth", split_axis=0, concat_axis=0, tiled=True)
    return left.astype(F32)[None]


def solution(mesh):
    in_specs = (
        P("depth", "probe", None, None),
        P("depth", "probe"),
        P("depth"),
        P("probe"),
        P(),
        P(),
    )
    out_specs = P("depth", "probe", None, None, None)
    return jax.shard_map(shards, mesh=mesh, in_specs=in_specs, out_specs=out_specs, check_vma=False)
```

```python
import functools
import math

import jax
import jax.numpy as jnp
from jax import lax
from jax.experimental import pallas as pl
from jax.experimental.pallas import tpu as pltpu
from jax.sharding import PartitionSpec as P

SLICE_MAX = 4
TCOLS = 8
TILES = SLICE_MAX * TCOLS
TILE = 128
N = 256
SIGMA = 0.7
CAP = 6
META = 16
POS_LANE = 8
CHUNKS = ((0, 96), (96, 32))
HALF = TILE // 2
SECTIONS = 4
SKIP = 64.0

BF16 = jnp.bfloat16
F32 = jnp.float32


def dft_tables(points):
    grid_index = jnp.arange(points, dtype=jnp.int32)
    angle_table = (grid_index[:, None] * grid_index[None, :] % points).astype(F32) * (
        2.0 * math.pi / points
    )
    norm_scale = 1.0 / math.sqrt(points)
    real_part = (jnp.cos(angle_table) * norm_scale).astype(BF16)
    imag_part = (-jnp.sin(angle_table) * norm_scale).astype(BF16)
    return (real_part, imag_part)


def whole(space=pltpu.VMEM):
    return pl.BlockSpec(memory_space=space)


def pieces(chunk):
    row0, rows = chunk
    parts = [(HALF + row0, 0, rows, 0)]
    if row0 < HALF:
        parts.append((HALF + TILE + row0, 0, min(HALF - row0, rows), -1))
    if row0 + rows > HALF:
        skipped = max(HALF - row0, 0)
        parts.append((row0 + skipped - HALF, skipped, rows - skipped, 1))
    return parts


def pack_kernel(row0, rows, tile_sm, pos_sm, blocks_hbm, tile_row, out, counts, sem):
    owners = out.shape[0]
    atoms = tile_row.shape[1]

    @pl.loop(0, owners)
    def _(o):
        counts[o] = 0

    @pl.loop(0, atoms, unroll=4)
    def _(a):
        o = lax.shift_right_logical(tile_sm[a], 5)
        r = counts[o]
        counts[o] = r + 1
        pltpu.make_async_copy(
            blocks_hbm.at[a, pl.ds(row0, rows), :],
            out.at[o, pl.ds(pl.multiple_of(r * rows, rows), rows), :],
            sem,
        ).start()

    shape = (atoms, atoms)
    t_row = jnp.broadcast_to(tile_row[...].astype(F32), shape)
    t_col = jnp.transpose(t_row).astype(jnp.int32)
    t_row = t_row.astype(jnp.int32)
    own_row = lax.shift_right_logical(t_row, 5)
    own_col = lax.shift_right_logical(t_col, 5)
    i_sub = lax.broadcasted_iota(jnp.int32, shape, 0)
    i_lane = lax.broadcasted_iota(jnp.int32, shape, 1)
    earlier = jnp.where((own_row == own_col) & (i_lane < i_sub), 1.0, 0.0)
    rank_col = jnp.sum(earlier, axis=1, keepdims=True).astype(jnp.int32)
    local = (t_col & (TILES - 1)) + 1
    slot_of = jnp.where(rank_col == i_lane, local.astype(F32), 0.0).astype(BF16)
    o_sub = lax.broadcasted_iota(jnp.int32, (owners, atoms), 0)
    o_lane = lax.broadcasted_iota(jnp.int32, (owners, atoms), 1)
    named = jnp.where(own_row[:owners] == o_sub, 1.0, 0.0).astype(BF16)
    meta = jnp.dot(named, slot_of, preferred_element_type=F32)
    for k in range(pos_sm.shape[0]):
        meta = jnp.where(o_lane == POS_LANE + k, pos_sm[k].astype(F32), meta)
    for o in range(owners):
        line = jnp.broadcast_to(meta[o : o + 1, :], (META, atoms))
        out[o, pl.ds(CAP * rows, META), :] = line.astype(BF16)
    moved = blocks_hbm.at[:, pl.ds(row0, rows), :]
    pltpu.make_async_copy(moved, moved, sem).wait()


def pack(blocks, tiles, positions, chunk, owners):
    atoms = blocks.shape[0]
    row0, rows = chunk
    return pl.pallas_call(
        functools.partial(pack_kernel, row0, rows),
        out_shape=jax.ShapeDtypeStruct((owners, CAP * rows + META, TILE), BF16),
        in_specs=[whole(pltpu.SMEM), whole(pltpu.SMEM), whole(pl.ANY), whole()],
        out_specs=whole(),
        scratch_shapes=[pltpu.SMEM((owners,), jnp.int32), pltpu.SemaphoreType.DMA],
        name=f"pack{row0}",
    )(tiles, positions, blocks, tiles.reshape(1, atoms))


TWO_PI_HI = 6.28125
TWO_PI_LO = 2.0 * math.pi - TWO_PI_HI


def sum_kernel(chunk, slices_sm, arrived, *refs):
    parts = pieces(chunk)
    outs = refs[: len(parts) * SECTIONS]
    acc, meta_v, meta_s, sem = refs[len(parts) * SECTIONS :]
    owners = arrived.shape[0]
    rows = chunk[1]
    meta_v[...] = arrived[:, CAP * rows, :].astype(F32).astype(jnp.int32)
    copy = pltpu.make_async_copy(meta_v, meta_s, sem)
    copy.start()
    acc[...] = jnp.zeros_like(acc)
    copy.wait()

    @pl.loop(0, owners)
    def _(o):
        for r in range(CAP):
            t = meta_s[o, r]
            acc[t] += arrived[o, pl.ds(r * rows, rows), :].astype(F32)

    count = slices_sm[0]
    me = lax.axis_index("probe")
    depth = lax.axis_index("depth")

    for index, (_, first, size, side) in enumerate(parts):
        target = lax.rem(me + side + owners, owners)
        for k in range(SECTIONS):
            ref = outs[index * SECTIONS + k]
            d = lax.rem(depth + k, SECTIONS)
            start = meta_s[target, POS_LANE + d]
            for h in range(2):
                column = lax.rem(start + h, TCOLS)

                @pl.loop(0, SLICE_MAX)
                def _(s):
                    angle = SIGMA * acc[1 + s * TCOLS + column, pl.ds(first, size), :]
                    turns = jnp.round(angle * (1.0 / (2.0 * math.pi)))
                    angle = (angle - turns * TWO_PI_HI) - turns * TWO_PI_LO
                    ref[s, h] = jnp.where(s < count, angle, SKIP).astype(BF16)


def sum_tiles(arrived, slice_count, chunk):
    owners = arrived.shape[0]
    parts = pieces(chunk)
    shapes = [
        jax.ShapeDtypeStruct((SLICE_MAX, 2, size, TILE), BF16)
        for _, _, size, _ in parts
        for _ in range(SECTIONS)
    ]
    flat = pl.pallas_call(
        functools.partial(sum_kernel, chunk),
        out_shape=shapes,
        in_specs=[whole(pltpu.SMEM), whole()],
        out_specs=[whole()] * len(shapes),
        scratch_shapes=[
            pltpu.VMEM((TILES + 1, chunk[1], TILE), F32),
            pltpu.VMEM((owners, TILE), jnp.int32),
            pltpu.SMEM((owners, TILE), jnp.int32),
            pltpu.SemaphoreType.DMA,
        ],
        name=f"sum{chunk[0]}",
    )(slice_count, arrived)
    return [flat[i * SECTIONS : (i + 1) * SECTIONS] for i in range(len(parts))]


SIN_C = (-1.6666654611e-1, 8.3321608736e-3, -1.9515295891e-4)
COS_C = (4.166664568298827e-2, -1.388731625493765e-3, 2.443315711809948e-5)


def sin_cos(angle):
    quarter = jnp.round(angle * (2.0 / math.pi))
    x = angle - quarter * (math.pi / 2.0)
    x2 = x * x
    s = x + x * x2 * (SIN_C[0] + x2 * (SIN_C[1] + x2 * SIN_C[2]))
    c = 1.0 - 0.5 * x2 + x2 * x2 * (COS_C[0] + x2 * (COS_C[1] + x2 * COS_C[2]))
    odd = jnp.abs(quarter) == 1.0
    sin_out = jnp.where(odd, c, s)
    cos_out = jnp.where(odd, s, c)
    sin_out = jnp.where((quarter == -1.0) | (jnp.abs(quarter) == 2.0), -sin_out, sin_out)
    cos_out = jnp.where((quarter == 1.0) | (jnp.abs(quarter) == 2.0), -cos_out, cos_out)
    return sin_out, cos_out


def waves_kernel(plan, wave_ref, phase_ref, m1, m2, *refs):
    count = len(plan)
    sources = refs[:count]
    out, psi, left, mid, rotor, window, sems = refs[count:]
    step = 32
    depth = lax.axis_index("depth")

    def copy_of(i):
        k, row, size, slot = plan[i]
        sec = lax.rem(depth + SECTIONS - k, SECTIONS)
        return pltpu.make_async_copy(
            sources[i], window.at[sec, :, :, pl.ds(row, size), :], sems.at[i]
        )

    for i in range(count):
        copy_of(i).start()

    for b in range(N // step):
        rows = pl.ds(b * step, step)
        for c in range(2):
            psi[rows, pl.ds(c * N, N)] = wave_ref[c, rows, :]
        s_out, c_out = sin_cos(phase_ref[rows, :])
        rotor[rows, pl.ds(0, N)] = c_out
        rotor[rows, pl.ds(N, N)] = s_out

    for i in range(count):
        copy_of(i).wait()

    def one_slice(sec, s):
        for b in range(N // step):
            rows = pl.ds(b * step, step)
            for h in range(2):
                s_out, c_out = sin_cos(window[sec, s, h, rows, :].astype(F32))
                re = psi[rows, pl.ds(h * TILE, TILE)]
                im = psi[rows, pl.ds(N + h * TILE, TILE)]
                lanes = pl.ds(h * TILE, TILE)
                left[rows, lanes] = (re * c_out - im * s_out).astype(BF16)
                left[pl.ds(N + b * step, step), lanes] = (re * s_out + im * c_out).astype(BF16)
        for c in range(2):
            half = jnp.dot(m1[pl.ds(c * N, N), :], left[...], preferred_element_type=F32)
            mid[:, pl.ds(c * N, N)] = half.astype(BF16)
        for b in range(2):
            half = N // 2
            rows = pl.ds(b * half, half)
            value = jnp.dot(mid[rows, :], m2[...], preferred_element_type=F32)
            re, im = value[:, :N], value[:, N:]
            cr, ci = rotor[rows, pl.ds(0, N)], rotor[rows, pl.ds(N, N)]
            left[rows, :] = (re * cr - im * ci).astype(BF16)
            left[pl.ds(N + b * half, half), :] = (re * ci + im * cr).astype(BF16)
        for c in range(2):
            half = jnp.dot(m2[pl.ds(c * N, N), :], left[...], preferred_element_type=F32)
            mid[:, pl.ds(c * N, N)] = half.astype(BF16)
        for b in range(2):
            half = N // 2
            rows = pl.ds(b * half, half)
            psi[rows, :] = jnp.dot(mid[rows, :], m1[...], preferred_element_type=F32)

    for sec in range(SECTIONS):

        @pl.loop(0, SLICE_MAX)
        def _(s):
            used = jnp.max(window[sec, s, 0, pl.ds(0, 16), :].astype(F32)) < SKIP / 2

            @pl.when(used)
            def _():
                one_slice(sec, s)

        for c in range(2):
            out[sec, c] = psi[:, pl.ds(c * N, N)].astype(BF16)


def run_waves(probe_wave, prop_phase, m1, m2, plan, windows):
    return pl.pallas_call(
        functools.partial(waves_kernel, plan),
        out_shape=jax.ShapeDtypeStruct((SECTIONS, 2, N, N), BF16),
        in_specs=[whole()] * 4 + [whole(pl.ANY)] * len(windows),
        out_specs=whole(),
        scratch_shapes=[
            pltpu.VMEM((N, 2 * N), F32),
            pltpu.VMEM((2 * N, N), BF16),
            pltpu.VMEM((N, 2 * N), BF16),
            pltpu.VMEM((N, 2 * N), F32),
            pltpu.VMEM((SECTIONS, SLICE_MAX, 2, N, TILE), BF16),
            pltpu.SemaphoreType.DMA((len(windows),)),
        ],
        name="waves",
    )(probe_wave, prop_phase, m1, m2, *windows)


def moved(x, k, side, sections, owners):
    if k == 0 and side == 0:
        return x
    route = [
        (
            d * owners + p,
            (d + k) % sections * owners + (p + side) % owners,
        )
        for d in range(sections)
        for p in range(owners)
    ]
    return lax.ppermute(x, ("depth", "probe"), route)


def shards(atom_blocks, atom_tile, slice_counts, positions, probe_wave, prop_phase):
    owners = lax.axis_size("probe")
    blocks = atom_blocks[0]
    tiles = atom_tile[0]
    plan, windows = [], []
    for chunk in CHUNKS:
        packed = pack(blocks, tiles, positions, chunk, owners)
        arrived = lax.all_to_all(packed, "probe", split_axis=0, concat_axis=0, tiled=True)
        groups = sum_tiles(arrived, slice_counts, chunk)
        for (row, _, size, side), group in zip(pieces(chunk), groups):
            for k in range(SECTIONS):
                plan.append((k, row, size, len(plan)))
                windows.append(moved(group[k], k, side, SECTIONS, owners))
    fr, fi = dft_tables(N)
    m1 = jnp.concatenate(
        [jnp.concatenate([fr, -fi], axis=1), jnp.concatenate([fi, fr], axis=1)], axis=0
    )
    m2 = jnp.concatenate(
        [jnp.concatenate([fr, fi], axis=1), jnp.concatenate([-fi, fr], axis=1)], axis=0
    )
    left = run_waves(probe_wave, prop_phase, m1, m2, tuple(plan), windows)
    left = lax.all_to_all(left, "depth", split_axis=0, concat_axis=0, tiled=True)
    return left.astype(F32)[None]


def solution(mesh):
    in_specs = (
        P("depth", "probe", None, None),
        P("depth", "probe"),
        P("depth"),
        P("probe"),
        P(),
        P(),
    )
    out_specs = P("depth", "probe", None, None, None)
    return jax.shard_map(shards, mesh=mesh, in_specs=in_specs, out_specs=out_specs, check_vma=False)
```
